128 devices in a mesh: dom: 8 (over x, core), blk: 16 (over z, y).
Axes of the slice: x: 4, y: 4, z: 4, core: 2. Of those that a mesh axis runs over, the one named last changes fastest.
Arguments:
- incident: bfloat16 [1024, 512, 192], P(('dom', 'blk')), may hold values from -6 to 6
- t_matrices: bfloat16 [1024, 512, 512], P(('dom', 'blk')), may hold values from -0.25 to 0.25
- translations: bfloat16 [4, 512, 512], replicated, may hold values from -0.125 to 0.125
- near_index: int32 [1024, 6], P(('dom', 'blk')), may hold values from 0 to 1023, as said below
- near_count: int32 [1024], P(('dom', 'blk')), may hold values from 1 to 6, as said below
- near_type: int32 [1024, 6], P(('dom', 'blk')), may hold values from 0 to 3
- phases: bfloat16 [1024, 2048], P(('dom', 'blk')), may hold values from -1 to 1
- wave_basis: bfloat16 [2048, 512], replicated, may hold values from -0.25 to 0.25
- grating_blocks: float32 [16, 128, 128], P('blk'), may hold values from -0.01171875 to 0.01171875
Outputs:
- coeffs: bfloat16 [1024, 512, 192], P(('dom', 'blk'))
The draws below stay inside these ranges and needn't reach their ends.
Inputs may be any that keep to these rules, and one draw needn't show every extreme that they name: `near_index`: the first near_count[p] entries of row p are distinct particles other than p, each within 4 of p, ascending; the remaining entries equal p and carry no weight. `near_count`: some particle has exactly 6 live neighbours.
All inputs are finite; a program needn't handle non-finite values.
Results may differ from the reference program's by a relative error of at most 0.015.
Values may be sent and summed in bfloat16 or wider, within the bound.
A program may use at most 64 MiB of HBM per device.

```python
import math
import jax
import jax.numpy as jnp
from jax import lax

L = 512
M = 192
G = 2048
BLOCK = 128
NT = 4
K = 6
ITERS = 2
REACH = 4
P_SIZE = 1024
NB = 16


def near_lists(key):
    first_key, second_key, third_key = jax.random.split(jax.random.fold_in(key, 7), 3)
    offsets = jnp.concatenate([jnp.arange(-REACH, 0), jnp.arange(1, REACH + 1)]).astype(jnp.int32)
    particle = jnp.arange(P_SIZE, dtype=jnp.int32)[:, None]
    candidate = particle + offsets[None, :]
    valid = (candidate >= 0) & (candidate < P_SIZE)
    valid_count = jnp.sum(valid.astype(jnp.int32), axis=1)
    raw_score = jax.random.randint(first_key, (P_SIZE, 2 * REACH), 0, 1 << 20)
    positions = jnp.arange(2 * REACH, dtype=jnp.int32)[None, :]
    score = jnp.where(valid, raw_score * (2 * REACH) + positions, -1 - positions)
    ranking = jnp.argsort(-score, axis=1, stable=True)
    counts = jax.random.randint(second_key, (P_SIZE,), 1, K + 1)
    forced = jax.random.randint(third_key, (), REACH, P_SIZE - REACH)
    counts = jnp.where(particle[:, 0] == forced, K, counts)
    counts = jnp.minimum(counts, valid_count)
    chosen = jnp.take_along_axis(candidate, ranking[:, :K], axis=1)
    live = jnp.arange(K, dtype=jnp.int32)[None, :] < counts[:, None]
    keyed = jnp.where(live, chosen, 2 * P_SIZE + jnp.arange(K, dtype=jnp.int32)[None, :])
    keyed = jnp.sort(keyed, axis=1)
    index = jnp.where(keyed < P_SIZE, keyed, particle)
    return (index.astype(jnp.int32), counts.astype(jnp.int32))


def draw_near_index(key, part):
    return near_lists(key)[0]


def draw_near_count(key, part):
    return near_lists(key)[1]


def set_ends(result, rng, low, top_value):
    longest = result.shape.index(max(result.shape))
    spots = []
    for shift in (0, 1):
        where = [jax.random.randint(jax.random.fold_in(rng, axis), (), 0, length) for axis, length in enumerate(result.shape)]
        where[longest] = (where[longest] + shift) % result.shape[longest]
        spots.append(tuple(where))
    return result.at[spots[0]].set(low).at[spots[1]].set(top_value)


def level_of(own_key, dims, cuts, least, high):
    loudness, own = 1.0, jax.random.fold_in(own_key, 6)
    for dim, blocks in cuts:
        steps = jnp.exp(jax.random.uniform(jax.random.fold_in(own, dim), (blocks,), jnp.float32, least / len(cuts), high / len(cuts)))
        loudness = loudness * jnp.repeat(steps, dims[dim] // blocks).reshape([-1 if axis == dim else 1 for axis in range(len(dims))])
    return loudness


def gaussian(own_key, extent, width, reach, cuts=(), kind=jnp.bfloat16):
    entries = jax.random.normal(own_key, extent, jnp.float32) * width
    if len(cuts) > 0:
        entries = level_of(own_key, extent, cuts, -0.22, 0.18) * entries
    return jnp.clip(entries, min=-reach, max=reach).astype(kind)


def setup_inputs(seed: int = 0) -> dict:
    key_list = jax.random.split(jax.random.key(seed), 10)
    return {
        "incident": gaussian(key_list[0], (P_SIZE, L, M), 1.0, 6.0, ((0, 128),)),
        "t_matrices": gaussian(key_list[1], (P_SIZE, L, L), L ** -0.5, 0.25, ((0, 128),)),
        "translations": gaussian(key_list[2], (NT, L, L), (4 * L) ** -0.5, 0.125),
        "near_index": draw_near_index(jax.random.fold_in(key_list[9], 71), 0),
        "near_count": draw_near_count(jax.random.fold_in(key_list[9], 71), 0),
        "near_type": set_ends(jax.random.randint(key_list[5], (P_SIZE, K), 0, NT), jax.random.fold_in(key_list[5], 1), 0, NT - 1).astype(jnp.int32),
        "phases": jnp.clip(jax.random.uniform(key_list[6], (P_SIZE, G), jnp.float32, -1.0, 1.0) * level_of(key_list[6], (P_SIZE, G), ((0, 128),), -0.4, 0.0), -1.0, 1.0).astype(jnp.bfloat16),
        "wave_basis": gaussian(key_list[7], (G, L), L ** -0.5, 0.25),
        "grating_blocks": gaussian(key_list[8], (NB, BLOCK, BLOCK), (2 * BLOCK * P_SIZE) ** -0.5, 0.01171875, ((0, 16),), jnp.float32),
    }


def rounded(values):
    return lax.optimization_barrier(values.astype(jnp.bfloat16)).astype(jnp.float32)


def solve_block(t_block, source):
    return jnp.einsum('pab,pbm->pam', t_block.astype(jnp.float32), source.astype(jnp.float32)).astype(jnp.bfloat16)


def reference(incident, t_matrices, translations, near_index, near_count, near_type, phases, wave_basis, grating_blocks):
    blocks = math.gcd(P_SIZE, 64)
    groups = P_SIZE // blocks

    def shaped(values):
        return values.reshape((groups, blocks) + values.shape[1:])

    basis = wave_basis.astype(jnp.float32)
    moves = translations.astype(jnp.float32)
    coeffs = lax.map(lambda pair: solve_block(pair[0], pair[1]), (shaped(t_matrices), shaped(incident))).reshape(P_SIZE, L, M)
    live = jnp.arange(K)[None, :] < near_count[:, None]
    for sweep in range(ITERS):
        def outward(total, pair):
            phase_block, coeff_block = pair
            spread = jnp.einsum('gl,plm->pgm', basis, coeff_block.astype(jnp.float32))
            return total + jnp.einsum('pg,pgm->gm', phase_block.astype(jnp.float32), spread), None

        sums, _ = lax.scan(outward, jnp.zeros((G, M), jnp.float32), (shaped(phases), shaped(coeffs)))
        reflected = jnp.einsum('bij,bjm->bim', grating_blocks.astype(jnp.float32), sums.reshape(NB, BLOCK, M), precision=lax.Precision.HIGHEST).reshape(G, M)
        reflected_wide = rounded(reflected)
        current = coeffs

        def update(items):
            t_block, inc_block, index_block, live_block, type_block, phase_block = items
            gathered = jnp.take(current, index_block, axis=0).astype(jnp.float32)
            weights = ((type_block[None] == jnp.arange(NT)[:, None, None]) & live_block[None]).astype(jnp.float32)
            grouped = rounded(jnp.einsum('tpk,pklm->tplm', weights, gathered))
            near_field = jnp.einsum('tab,tpbm->pam', moves, grouped)
            weighted = rounded(phase_block.astype(jnp.float32)[:, :, None] * reflected_wide[None])
            returned = jnp.einsum('gl,pgm->plm', basis, weighted)
            source = rounded(inc_block.astype(jnp.float32) + near_field + returned)
            return solve_block(t_block, source)

        coeffs = lax.map(update, (shaped(t_matrices), shaped(incident), shaped(near_index), shaped(live), shaped(near_type), shaped(phases))).reshape(P_SIZE, L, M)
    return coeffs
```

```python
import functools

import jax
import jax.numpy as jnp
from jax import lax
from jax.experimental import pallas as pl
from jax.experimental.pallas import tpu as pltpu
from jax.sharding import PartitionSpec as P

ITERS = 2
F32 = jnp.float32
BF16 = jnp.bfloat16
NT_DIMS = (((1,), (1,)), ((), ()))
NN_DIMS = (((1,), (0,)), ((), ()))


def dot(a, b, dims, precision=None):
    return lax.dot_general(a, b, dims, precision=precision, preferred_element_type=F32)


def kernel(
    xs,
    table_ref,
    incident_hbm,
    t_hbm,
    moves_hbm,
    phases_ref,
    basis_hbm,
    grating_ref,
    out_hbm,
    inc_stage,
    out_stage,
    inc_ref,
    t_ref,
    moves_ref,
    basis_ref,
    win,
    halo,
    acc,
    src,
    steps,
    groups,
    pair_out,
    pair_in,
    x_out,
    x_in,
    b_out,
    b_in,
    refl,
    inc_sem,
    t_sem,
    load_sem,
    out_sem,
    pair_s,
    pair_r,
    x_s,
    x_r,
    b_s,
    b_r,
    a_s,
    a_r,
    x2_s,
    x2_r,
    p2_s,
    p2_r,
    halo_s,
    halo_r,
):
    count, _, rows_m = inc_stage.shape
    reach = count // 2
    kinds = moves_ref.shape[0]
    most = (table_ref.shape[1] - kinds) // 2
    width = basis_ref.shape[1]
    total = basis_ref.shape[0]
    half = total // 2
    chunk = half // 2
    order = grating_ref.shape[1]
    doms, blks = 2 * xs, total // order
    per_half = blks // 2
    per_chunk = per_half // 2
    part = rows_m // xs

    dom = lax.axis_index("dom")
    blk = lax.axis_index("blk")
    x, core = dom // 2, dom % 2
    partner = x * 2 + (1 - core)
    linear = dom * blks + blk
    after = lax.rem(linear + 1, doms * blks)
    before = lax.rem(linear + doms * blks - 1, doms * blks)
    after_id = (after // blks, lax.rem(after, blks))
    before_id = (before // blks, lax.rem(before, blks))
    is_owner = blk // per_half == core

    def peer_x(d):
        return lax.rem(x + d, xs) * 2 + core

    def remote(source, target, send, recv, device):
        return pltpu.make_async_remote_copy(
            src_ref=source,
            dst_ref=target,
            send_sem=send,
            recv_sem=recv,
            device_id=device,
            device_id_type=pl.DeviceIdType.MESH,
        )

    def solve_order(i):
        return jnp.where(lax.rem(i, 2) == 0, count - 1 - i // 2, i // 2)

    def inc_load(p):
        return pltpu.make_async_copy(incident_hbm.at[p], inc_stage.at[p], inc_sem.at[p])

    def t_load(p):
        return pltpu.make_async_copy(t_hbm.at[p], t_ref.at[p], t_sem.at[p])

    @pl.loop(0, count)
    def _(i):
        p = solve_order(i)
        inc_load(p).start()
        t_load(p).start()

    basis_load = pltpu.make_async_copy(basis_hbm, basis_ref, load_sem.at[0])
    moves_load = pltpu.make_async_copy(moves_hbm, moves_ref, load_sem.at[1])
    basis_load.start()
    moves_load.start()

    barrier = pltpu.get_barrier_semaphore()

    def greet(device):
        pl.semaphore_signal(
            barrier, inc=1, device_id=device, device_id_type=pl.DeviceIdType.MESH
        )

    greet((partner, blk))
    for d in range(1, xs):
        greet((peer_x(d), blk))

    @pl.loop(1, blks)
    def _(o):
        greet((dom, lax.rem(blk + o, blks)))

    greet(after_id)
    greet(before_id)

    steps[most] = jnp.zeros((rows_m, width), BF16)

    def halo_copy(s, i, to_after):
        if to_after:
            return remote(
                win.at[2 * reach + i], halo.at[s, i], halo_s.at[s, i], halo_r.at[s, i], after_id
            )
        return remote(
            win.at[reach + i],
            halo.at[s, reach + i],
            halo_s.at[s, reach + i],
            halo_r.at[s, reach + i],
            before_id,
        )

    def halo_send(s, batch):
        halo_copy(s, reach - 1 - batch, True).start()
        halo_copy(s, batch, False).start()

    def solve_first(i, carry):
        p = solve_order(i)
        inc_load(p).wait()
        t_load(p).wait()
        turned = inc_stage[p].T
        inc_ref[p] = turned
        win[reach + p] = dot(turned, t_ref[p], NT_DIMS).astype(BF16)
        return carry

    lax.fori_loop(0, reach, solve_first, 0)
    pl.semaphore_wait(barrier, blks - 1 + xs - 1 + 1 + 2)
    for batch in range(reach // 2):
        halo_send(0, batch)
    lax.fori_loop(reach, count, solve_first, 0)

    basis_load.wait()

    def near_field(s, batch):
        lo, hi = reach - 1 - batch, reach + batch
        halo_copy(s, reach - 1 - batch, True).wait_recv()
        halo_copy(s, batch, False).wait_recv()
        win[reach - 1 - batch] = halo[s, reach - 1 - batch]
        win[3 * reach + batch] = halo[s, reach + batch]
        piece = 32 if rows_m % 32 == 0 else rows_m
        for place, p in enumerate((lo, hi)):
            index = [table_ref[p, k] for k in range(most)]
            same = [table_ref[p, most + k].astype(F32) for k in range(most)]
            ends = [table_ref[p, 2 * most + t] for t in range(kinds)]

            @pl.loop(0, rows_m // piece)
            def _(r):
                rows = pl.ds(pl.multiple_of(r * piece, piece), piece)
                run = win[index[0], rows, :].astype(F32)
                steps[0, rows, :] = run.astype(BF16)
                for k in range(1, most):
                    run = run * same[k] + win[index[k], rows, :].astype(F32)
                    steps[k, rows, :] = run.astype(BF16)

            for t in range(kinds):
                groups[t, place * rows_m : (place + 1) * rows_m, :] = steps[ends[t]]
        field = dot(groups[0], moves_ref[0], NT_DIMS)
        for t in range(1, kinds):
            field = field + dot(groups[t], moves_ref[t], NT_DIMS)
        for place, p in enumerate((lo, hi)):
            acc[p] = inc_ref[p].astype(F32) + field[place * rows_m : (place + 1) * rows_m]

    my_rows = pl.ds(pl.multiple_of(x * part, part), part)

    def outward(start):
        cols = pl.ds(pl.multiple_of(start, chunk), chunk)
        spread = dot(
            win[reach : reach + count].reshape(count * rows_m, width), basis_ref[cols, :], NT_DIMS
        ).reshape(count, rows_m, chunk)
        return jnp.sum(spread * phases_ref[:, :, cols].astype(F32), axis=0)

    def inward(s, start, last):
        cols = pl.ds(pl.multiple_of(start, chunk), chunk)
        weighted = (refl[s, :, cols][None] * phases_ref[:, :, cols]).reshape(count * rows_m, chunk)
        back = dot(weighted, basis_ref[cols, :], NN_DIMS).reshape(count, rows_m, width)
        if last:
            src[...] = (acc[...] + back).astype(BF16)
        else:
            acc[...] += back

    def pair_copy(s, j):
        cols = pl.ds(pl.multiple_of(j * chunk, chunk), chunk)
        return remote(
            pair_out.at[s, :, cols],
            pair_in.at[s, :, cols],
            pair_s.at[s, j],
            pair_r.at[s, j],
            (partner, blk),
        )

    def x_copy(s, j, d):
        cols = pl.ds(pl.multiple_of(j * chunk, chunk), chunk)
        their = pl.ds(pl.multiple_of(lax.rem(x + d, xs) * part, part), part)
        return remote(
            x_out.at[s, their, cols],
            x_in.at[s, d - 1, :, cols],
            x_s.at[s, j, d - 1],
            x_r.at[s, j, d - 1],
            (peer_x(d), blk),
        )

    def b_copy(s, b):
        cols = pl.ds(pl.multiple_of(b * order, order), order)
        return remote(
            b_out.at[s, :, cols],
            b_in.at[s, blk],
            b_s.at[s, b],
            b_r.at[s, blk],
            (dom, core * per_half + b),
        )

    def b_arrival(s, sender):
        return remote(
            b_out.at[s, :, pl.ds(0, order)],
            b_in.at[s, sender],
            b_s.at[s, 0],
            b_r.at[s, sender],
            (dom, sender),
        )

    def refl_at(s, b):
        cols = pl.ds(pl.multiple_of((core * per_half + b) * order, order), order)
        return refl.at[s, my_rows, cols]

    mine = lax.rem(blk, per_half)

    def a_copy(s, o):
        return remote(
            refl_at(s, mine),
            refl_at(s, mine),
            a_s.at[s, o],
            a_r.at[s, mine],
            (dom, lax.rem(blk + o, blks)),
        )

    def a_arrival(s, b):
        return remote(
            refl_at(s, b), refl_at(s, b), a_s.at[s, 0], a_r.at[s, b], (dom, core * per_half + b)
        )

    def x2_copy(s, d, b):
        return remote(
            refl_at(s, b),
            refl_at(s, b),
            x2_s.at[s, d - 1, b],
            x2_r.at[s, d - 1, b],
            (peer_x(d), blk),
        )

    def x2_arrival(s, d, b):
        theirs = pl.ds(pl.multiple_of(lax.rem(x + xs - d, xs) * part, part), part)
        cols = pl.ds(pl.multiple_of((core * per_half + b) * order, order), order)
        place = refl.at[s, theirs, cols]
        return remote(
            place, place, x2_s.at[s, d - 1, b], x2_r.at[s, d - 1, b], (peer_x(xs - d), blk)
        )

    def p2_copy(s, j, sender):
        cols = pl.ds(pl.multiple_of(sender * half + j * chunk, chunk), chunk)
        return remote(
            refl.at[s, :, cols], refl.at[s, :, cols], p2_s.at[s, j], p2_r.at[s, j], (partner, blk)
        )

    @pl.loop(0, ITERS)
    def _(s):
        @pl.loop(0, 2)
        def _(j):
            cols = pl.ds(pl.multiple_of(j * chunk, chunk), chunk)
            pair_out[s, :, cols] = outward((1 - core) * half + j * chunk).astype(BF16)
            pair_copy(s, j).start()

        @pl.loop(0, 2)
        def _(j):
            cols = pl.ds(pl.multiple_of(j * chunk, chunk), chunk)
            own = outward(core * half + j * chunk)
            pair_copy(s, j).wait_recv()
            x_out[s, :, cols] = (own + pair_in[s, :, cols].astype(F32)).astype(BF16)
            for d in range(1, xs):
                x_copy(s, j, d).start()

        @pl.when(s == 0)
        def _():
            moves_load.wait()

        near_field(s, 0)

        @pl.loop(0, 2)
        def _(j):
            cols = pl.ds(pl.multiple_of(j * chunk, chunk), chunk)
            both = x_out[s, my_rows, cols].astype(F32)
            for d in range(1, xs):
                x_copy(s, j, d).wait_recv()
                both = both + x_in[s, d - 1, :, cols].astype(F32)
            b_out[s, :, cols] = both.astype(BF16)

            @pl.loop(0, per_chunk)
            def _(i):
                b = j * per_chunk + i

                @pl.when(core * per_half + b != blk)
                def _():
                    b_copy(s, b).start()

        halo_send(s, 2)
        near_field(s, 1)

        @pl.when(is_owner)
        def _():
            own_cols = pl.ds(pl.multiple_of(mine * order, order), order)

            def gather(o, so_far):
                sender = lax.rem(blk + o, blks)
                b_arrival(s, sender).wait_recv()
                return so_far + b_in[s, sender].astype(F32)

            sums = lax.fori_loop(1, blks, gather, b_out[s, :, own_cols].astype(F32))
            result = dot(sums, grating_ref[0], NT_DIMS, lax.Precision.HIGHEST)
            out_cols = pl.ds(pl.multiple_of(blk * order, order), order)
            refl[s, my_rows, out_cols] = result.astype(BF16)

            @pl.loop(1, blks)
            def _(o):
                a_copy(s, o).start()

        halo_send(s, 3)
        near_field(s, 2)

        @pl.loop(0, per_half)
        def _(o):
            b = lax.rem(mine + o, per_half)

            @pl.when(core * per_half + b != blk)
            def _():
                a_arrival(s, b).wait_recv()

            for d in range(1, xs):
                x2_copy(s, d, b).start()

        near_field(s, 3)

        for j in range(2):

            @pl.loop(0, per_chunk)
            def _(i):
                b = j * per_chunk + i
                for d in range(1, xs):
                    x2_arrival(s, d, b).wait_recv()

            p2_copy(s, j, core).start()
        for j in range(2):
            inward(s, core * half + j * chunk, False)
        for j in range(2):
            p2_copy(s, j, 1 - core).wait_recv()
            inward(s, (1 - core) * half + j * chunk, j == 1)

        for i in range(reach):
            halo_copy(s, i, True).wait_send()
            halo_copy(s, i, False).wait_send()
        for j in range(2):
            pair_copy(s, j).wait_send()
            p2_copy(s, j, core).wait_send()
            for d in range(1, xs):
                x_copy(s, j, d).wait_send()

        @pl.loop(0, per_half)
        def _(b):
            for d in range(1, xs):
                x2_copy(s, d, b).wait_send()

            @pl.when(core * per_half + b != blk)
            def _():
                b_copy(s, b).wait_send()

        @pl.when(is_owner)
        def _():
            @pl.loop(1, blks)
            def _(o):
                a_copy(s, o).wait_send()

        @pl.when(s < ITERS - 1)
        def _():
            def solve_next(i, carry):
                p = solve_order(i)
                win[reach + p] = dot(src[p], t_ref[p], NT_DIMS).astype(BF16)
                return carry

            lax.fori_loop(0, reach, solve_next, 0)
            for batch in range(reach // 2):
                halo_send(s + 1, batch)
            lax.fori_loop(reach, count, solve_next, 0)

    def out_copy(p):
        return pltpu.make_async_copy(out_stage.at[p], out_hbm.at[p], out_sem.at[p])

    @pl.loop(0, count)
    def _(p):
        out_stage[p] = dot(t_ref[p], src[p], NT_DIMS).astype(BF16)
        out_copy(p).start()

    @pl.loop(0, count)
    def _(p):
        out_copy(p).wait()


def slot_table(near_index, near_count, near_type, first, kinds, reach):
    most = near_index.shape[1]
    place = jnp.arange(most)
    slots = near_index - first + reach
    key = jnp.where(place[None, :] < near_count[:, None], near_type, kinds)
    ahead = (key[:, :, None] < key[:, None, :]) | (
        (key[:, :, None] == key[:, None, :]) & (place[:, None] < place[None, :])[None]
    )
    rank = jnp.sum(ahead.astype(jnp.int32), axis=1)
    hit = (rank[:, :, None] == place[None, None, :]).astype(jnp.int32)
    index = jnp.sum(hit * slots[:, :, None], axis=1)
    key_sorted = jnp.sum(hit * key[:, :, None], axis=1)
    same = jnp.concatenate(
        [jnp.zeros_like(key[:, :1]), (key_sorted[:, 1:] == key_sorted[:, :-1]).astype(jnp.int32)],
        axis=1,
    )
    kind = jnp.arange(kinds)[None, None, :]
    upto = jnp.sum((key[:, :, None] <= kind).astype(jnp.int32), axis=1)
    some = jnp.any(key[:, :, None] == kind, axis=1)
    ends = jnp.where(some, upto - 1, most)
    return jnp.concatenate([index, same, ends], axis=1).astype(jnp.int32)


def local(
    incident,
    t_matrices,
    translations,
    near_index,
    near_count,
    near_type,
    phases,
    wave_basis,
    grating_blocks,
):
    doms, blks = lax.axis_size("dom"), lax.axis_size("blk")
    xs = doms // 2
    count, width, rows_m = incident.shape
    reach = count // 2
    kinds = translations.shape[0]
    most = near_index.shape[1]
    total = wave_basis.shape[0]
    half = total // 2
    order = grating_blocks.shape[1]
    part = rows_m // xs
    per_half = blks // 2
    first = lax.axis_index(("dom", "blk")) * count
    table = slot_table(near_index, near_count, near_type, first, kinds, reach)
    hbm = pl.BlockSpec(memory_space=pl.ANY)
    vmem = pl.BlockSpec(memory_space=pltpu.VMEM)
    sem = pltpu.SemaphoreType.DMA
    n = ITERS
    return pl.pallas_call(
        functools.partial(kernel, xs),
        out_shape=jax.ShapeDtypeStruct(incident.shape, BF16),
        in_specs=[pl.BlockSpec(memory_space=pltpu.SMEM), hbm, hbm, hbm, vmem, hbm, vmem],
        out_specs=hbm,
        scratch_shapes=[
            pltpu.VMEM((count, width, rows_m), BF16),
            pltpu.VMEM((count, width, rows_m), BF16),
            pltpu.VMEM((count, rows_m, width), BF16),
            pltpu.VMEM((count, width, width), BF16),
            pltpu.VMEM((kinds, width, width), BF16),
            pltpu.VMEM((total, width), BF16),
            pltpu.VMEM((count + 2 * reach, rows_m, width), BF16),
            pltpu.VMEM((n, 2 * reach, rows_m, width), BF16),
            pltpu.VMEM((count, rows_m, width), F32),
            pltpu.VMEM((count, rows_m, width), BF16),
            pltpu.VMEM((most + 1, rows_m, width), BF16),
            pltpu.VMEM((kinds, 2 * rows_m, width), BF16),
            pltpu.VMEM((n, rows_m, half), BF16),
            pltpu.VMEM((n, rows_m, half), BF16),
            pltpu.VMEM((n, rows_m, half), BF16),
            pltpu.VMEM((n, xs - 1, part, half), BF16),
            pltpu.VMEM((n, part, half), BF16),
            pltpu.VMEM((n, blks, part, order), BF16),
            pltpu.VMEM((n, rows_m, total), BF16),
            sem((count,)),
            sem((count,)),
            sem((2,)),
            sem((count,)),
            sem((n, 2)),
            sem((n, 2)),
            sem((n, 2, xs - 1)),
            sem((n, 2, xs - 1)),
            sem((n, per_half)),
            sem((n, blks)),
            sem((n, blks)),
            sem((n, per_half)),
            sem((n, xs - 1, per_half)),
            sem((n, xs - 1, per_half)),
            sem((n, 2)),
            sem((n, 2)),
            sem((n, 2 * reach)),
            sem((n, 2 * reach)),
        ],
        compiler_params=pltpu.CompilerParams(
            collective_id=0, has_side_effects=True, vmem_limit_bytes=60 * 2**20
        ),
    )(
        table,
        incident,
        t_matrices,
        translations,
        phases.reshape(count, 1, total),
        wave_basis,
        grating_blocks,
    )


def solution(mesh):
    placed = (
        P(("dom", "blk"), None, None),
        P(("dom", "blk"), None, None),
        P(),
        P(("dom", "blk"), None),
        P(("dom", "blk")),
        P(("dom", "blk"), None),
        P(("dom", "blk"), None),
        P(),
        P("blk", None, None),
    )
    return jax.shard_map(
        local, mesh=mesh, in_specs=placed, out_specs=P(("dom", "blk"), None, None), check_vma=False
    )
```

```python
import functools

import jax
import jax.numpy as jnp
from jax import lax
from jax.experimental import pallas as pl
from jax.experimental.pallas import tpu as pltpu
from jax.sharding import PartitionSpec as P

ITERS = 2
F32 = jnp.float32
BF16 = jnp.bfloat16
NT_DIMS = (((1,), (1,)), ((), ()))
NN_DIMS = (((1,), (0,)), ((), ()))


def dot(a, b, dims, precision=None):
    return lax.dot_general(a, b, dims, precision=precision, preferred_element_type=F32)


def kernel(
    xs,
    index_ref,
    count_ref,
    type_ref,
    incident_hbm,
    t_hbm,
    moves_hbm,
    phases_hbm,
    basis_hbm,
    grating_hbm,
    out_hbm,
    table_ref,
    phases_flat,
    phases_ref,
    grating_ref,
    inc_ref,
    out_stage,
    t_ref,
    moves_ref,
    basis_ref,
    win,
    halo,
    acc,
    src,
    steps,
    groups,
    pair_out,
    pair_in,
    x_out,
    x_in,
    b_out,
    b_in,
    refl,
    inc_sem,
    t_sem,
    load_sem,
    out_sem,
    pair_s,
    pair_r,
    x_s,
    x_r,
    b_s,
    b_r,
    a_s,
    a_r,
    x2_s,
    x2_r,
    p2_s,
    p2_r,
    halo_s,
    halo_r,
):
    count, rows_m, _ = inc_ref.shape
    reach = count // 2
    kinds = moves_ref.shape[0]
    most = index_ref.shape[1]
    width = basis_ref.shape[1]
    total = basis_ref.shape[0]
    half = total // 2
    chunk = half // 2
    order = grating_ref.shape[1]
    doms, blks = 2 * xs, total // order
    per_half = blks // 2
    per_chunk = per_half // 2
    part = rows_m // xs

    dom = lax.axis_index("dom")
    blk = lax.axis_index("blk")
    x, core = dom // 2, dom % 2
    partner = x * 2 + (1 - core)
    linear = dom * blks + blk
    after = lax.rem(linear + 1, doms * blks)
    before = lax.rem(linear + doms * blks - 1, doms * blks)
    after_id = (after // blks, lax.rem(after, blks))
    before_id = (before // blks, lax.rem(before, blks))
    is_owner = blk // per_half == core

    def peer_x(d):
        return lax.rem(x + d, xs) * 2 + core

    def remote(source, target, send, recv, device):
        return pltpu.make_async_remote_copy(
            src_ref=source,
            dst_ref=target,
            send_sem=send,
            recv_sem=recv,
            device_id=device,
            device_id_type=pl.DeviceIdType.MESH,
        )

    def solve_order(i):
        return jnp.where(lax.rem(i, 2) == 0, count - 1 - i // 2, i // 2)

    def inc_load(p):
        return pltpu.make_async_copy(incident_hbm.at[p], inc_ref.at[p], inc_sem.at[p])

    def t_load(p):
        return pltpu.make_async_copy(t_hbm.at[p], t_ref.at[p], t_sem.at[p])

    @pl.loop(0, count)
    def _(i):
        p = solve_order(i)
        inc_load(p).start()
        t_load(p).start()

    basis_load = pltpu.make_async_copy(basis_hbm, basis_ref, load_sem.at[0])
    moves_load = pltpu.make_async_copy(moves_hbm, moves_ref, load_sem.at[1])
    phases_load = pltpu.make_async_copy(phases_hbm, phases_flat, load_sem.at[2])
    grating_load = pltpu.make_async_copy(grating_hbm, grating_ref, load_sem.at[3])
    phases_load.start()
    grating_load.start()
    basis_load.start()
    moves_load.start()

    barrier = pltpu.get_barrier_semaphore()

    def greet(device):
        pl.semaphore_signal(
            barrier, inc=1, device_id=device, device_id_type=pl.DeviceIdType.MESH
        )

    greet((partner, blk))
    for d in range(1, xs):
        greet((peer_x(d), blk))

    @pl.loop(1, blks)
    def _(o):
        greet((dom, lax.rem(blk + o, blks)))

    greet(after_id)
    greet(before_id)

    steps[most] = jnp.zeros((rows_m, width), BF16)

    @pl.loop(0, count)
    def _(p):
        live = count_ref[p]
        slot = [
            jnp.clip(index_ref[p, k] - linear * count + reach, 0, count + 2 * reach - 1)
            for k in range(most)
        ]
        key = [jnp.where(k < live, type_ref[p, k], kinds) for k in range(most)]
        rank = [jnp.int32(0)] * most
        for k in range(most):
            for n in range(k + 1, most):
                later = (key[n] < key[k]).astype(jnp.int32)
                rank[k] = rank[k] + later
                rank[n] = rank[n] + (1 - later)
        sorted_slot, sorted_key = [], []
        for r in range(most):
            here, kind = slot[0], key[0]
            for k in range(1, most):
                hit = rank[k] == r
                here = jnp.where(hit, slot[k], here)
                kind = jnp.where(hit, key[k], kind)
            sorted_slot.append(here)
            sorted_key.append(kind)
        for r in range(most):
            table_ref[p, r] = sorted_slot[r]
            if r > 0:
                table_ref[p, most + r] = (sorted_key[r] == sorted_key[r - 1]).astype(jnp.int32)
        for t in range(kinds):
            last = jnp.int32(most)
            for r in range(most):
                last = jnp.where(sorted_key[r] == t, r, last)
            table_ref[p, 2 * most + t] = last

    def halo_copy(s, i, to_after):
        if to_after:
            return remote(
                win.at[2 * reach + i], halo.at[s, i], halo_s.at[s, i], halo_r.at[s, i], after_id
            )
        return remote(
            win.at[reach + i],
            halo.at[s, reach + i],
            halo_s.at[s, reach + i],
            halo_r.at[s, reach + i],
            before_id,
        )

    def halo_send(s, batch):
        halo_copy(s, reach - 1 - batch, True).start()
        halo_copy(s, batch, False).start()

    def solve_first(i, carry):
        p = solve_order(i)
        inc_load(p).wait()
        t_load(p).wait()
        win[reach + p] = dot(inc_ref[p], t_ref[p], NT_DIMS).astype(BF16)
        return carry

    lax.fori_loop(0, reach, solve_first, 0)
    pl.semaphore_wait(barrier, blks - 1 + xs - 1 + 1 + 2)
    for batch in range(reach // 2):
        halo_send(0, batch)
    lax.fori_loop(reach, count, solve_first, 0)

    phases_load.wait()
    for p in range(count):
        phases_ref[p] = phases_flat[p : p + 1, :]
    basis_load.wait()

    def near_field(s, batch):
        lo, hi = reach - 1 - batch, reach + batch
        halo_copy(s, reach - 1 - batch, True).wait_recv()
        halo_copy(s, batch, False).wait_recv()
        win[reach - 1 - batch] = halo[s, reach - 1 - batch]
        win[3 * reach + batch] = halo[s, reach + batch]
        piece = 32 if rows_m % 32 == 0 else rows_m
        for place, p in enumerate((lo, hi)):
            index = [table_ref[p, k] for k in range(most)]
            same = [table_ref[p, most + k].astype(F32) if k else None for k in range(most)]
            ends = [table_ref[p, 2 * most + t] for t in range(kinds)]

            @pl.loop(0, rows_m // piece)
            def _(r):
                rows = pl.ds(pl.multiple_of(r * piece, piece), piece)
                run = win[index[0], rows, :].astype(F32)
                steps[0, rows, :] = run.astype(BF16)
                for k in range(1, most):
                    run = run * same[k] + win[index[k], rows, :].astype(F32)
                    steps[k, rows, :] = run.astype(BF16)

            for t in range(kinds):
                groups[t, place * rows_m : (place + 1) * rows_m, :] = steps[ends[t]]
        field = dot(groups[0], moves_ref[0], NT_DIMS)
        for t in range(1, kinds):
            field = field + dot(groups[t], moves_ref[t], NT_DIMS)
        for place, p in enumerate((lo, hi)):
            acc[p] = inc_ref[p].astype(F32) + field[place * rows_m : (place + 1) * rows_m]

    my_rows = pl.ds(pl.multiple_of(x * part, part), part)

    def outward(start):
        cols = pl.ds(pl.multiple_of(start, chunk), chunk)
        spread = dot(
            win[reach : reach + count].reshape(count * rows_m, width), basis_ref[cols, :], NT_DIMS
        ).reshape(count, rows_m, chunk)
        return jnp.sum(spread * phases_ref[:, :, cols].astype(F32), axis=0)

    def inward(s, start, last):
        cols = pl.ds(pl.multiple_of(start, chunk), chunk)
        weighted = (refl[s, :, cols][None] * phases_ref[:, :, cols]).reshape(count * rows_m, chunk)
        back = dot(weighted, basis_ref[cols, :], NN_DIMS).reshape(count, rows_m, width)
        if last:
            src[...] = (acc[...] + back).astype(BF16)
        else:
            acc[...] += back

    def pair_copy(s, j):
        cols = pl.ds(pl.multiple_of(j * chunk, chunk), chunk)
        return remote(
            pair_out.at[s, :, cols],
            pair_in.at[s, :, cols],
            pair_s.at[s, j],
            pair_r.at[s, j],
            (partner, blk),
        )

    def x_copy(s, j, d):
        cols = pl.ds(pl.multiple_of(j * chunk, chunk), chunk)
        their = pl.ds(pl.multiple_of(lax.rem(x + d, xs) * part, part), part)
        return remote(
            x_out.at[s, their, cols],
            x_in.at[s, d - 1, :, cols],
            x_s.at[s, j, d - 1],
            x_r.at[s, j, d - 1],
            (peer_x(d), blk),
        )

    def b_copy(s, b):
        cols = pl.ds(pl.multiple_of(b * order, order), order)
        return remote(
            b_out.at[s, :, cols],
            b_in.at[s, blk],
            b_s.at[s, b],
            b_r.at[s, blk],
            (dom, core * per_half + b),
        )

    def b_arrival(s, sender):
        return remote(
            b_out.at[s, :, pl.ds(0, order)],
            b_in.at[s, sender],
            b_s.at[s, 0],
            b_r.at[s, sender],
            (dom, sender),
        )

    def refl_at(s, b):
        cols = pl.ds(pl.multiple_of((core * per_half + b) * order, order), order)
        return refl.at[s, my_rows, cols]

    mine = lax.rem(blk, per_half)

    def a_copy(s, o):
        return remote(
            refl_at(s, mine),
            refl_at(s, mine),
            a_s.at[s, o],
            a_r.at[s, mine],
            (dom, lax.rem(blk + o, blks)),
        )

    def a_arrival(s, b):
        return remote(
            refl_at(s, b), refl_at(s, b), a_s.at[s, 0], a_r.at[s, b], (dom, core * per_half + b)
        )

    def x2_copy(s, d, b):
        return remote(
            refl_at(s, b),
            refl_at(s, b),
            x2_s.at[s, d - 1, b],
            x2_r.at[s, d - 1, b],
            (peer_x(d), blk),
        )

    def x2_arrival(s, d, b):
        theirs = pl.ds(pl.multiple_of(lax.rem(x + xs - d, xs) * part, part), part)
        cols = pl.ds(pl.multiple_of((core * per_half + b) * order, order), order)
        place = refl.at[s, theirs, cols]
        return remote(
            place, place, x2_s.at[s, d - 1, b], x2_r.at[s, d - 1, b], (peer_x(xs - d), blk)
        )

    def p2_copy(s, j, sender):
        cols = pl.ds(pl.multiple_of(sender * half + j * chunk, chunk), chunk)
        return remote(
            refl.at[s, :, cols], refl.at[s, :, cols], p2_s.at[s, j], p2_r.at[s, j], (partner, blk)
        )

    @pl.loop(0, ITERS)
    def _(s):
        @pl.loop(0, 2)
        def _(j):
            cols = pl.ds(pl.multiple_of(j * chunk, chunk), chunk)
            pair_out[s, :, cols] = outward((1 - core) * half + j * chunk).astype(BF16)
            pair_copy(s, j).start()

        @pl.loop(0, 2)
        def _(j):
            cols = pl.ds(pl.multiple_of(j * chunk, chunk), chunk)
            own = outward(core * half + j * chunk)
            pair_copy(s, j).wait_recv()
            x_out[s, :, cols] = (own + pair_in[s, :, cols].astype(F32)).astype(BF16)
            for d in range(1, xs):
                x_copy(s, j, d).start()

        @pl.when(s == 0)
        def _():
            moves_load.wait()
            grating_load.wait()

        near_field(s, 0)

        @pl.loop(0, 2)
        def _(j):
            cols = pl.ds(pl.multiple_of(j * chunk, chunk), chunk)
            both = x_out[s, my_rows, cols].astype(F32)
            for d in range(1, xs):
                x_copy(s, j, d).wait_recv()
                both = both + x_in[s, d - 1, :, cols].astype(F32)
            b_out[s, :, cols] = both.astype(BF16)

            @pl.loop(0, per_chunk)
            def _(i):
                b = j * per_chunk + i

                @pl.when(core * per_half + b != blk)
                def _():
                    b_copy(s, b).start()

        halo_send(s, 2)
        near_field(s, 1)

        @pl.when(is_owner)
        def _():
            own_cols = pl.ds(pl.multiple_of(mine * order, order), order)

            def gather(o, so_far):
                sender = lax.rem(blk + o, blks)
                b_arrival(s, sender).wait_recv()
                return so_far + b_in[s, sender].astype(F32)

            sums = lax.fori_loop(1, blks, gather, b_out[s, :, own_cols].astype(F32))
            result = dot(sums, grating_ref[0], NT_DIMS, lax.Precision.HIGHEST)
            out_cols = pl.ds(pl.multiple_of(blk * order, order), order)
            refl[s, my_rows, out_cols] = result.astype(BF16)

            @pl.loop(1, blks)
            def _(o):
                a_copy(s, o).start()

        halo_send(s, 3)
        near_field(s, 2)

        @pl.loop(0, per_half)
        def _(o):
            b = lax.rem(mine + o, per_half)

            @pl.when(core * per_half + b != blk)
            def _():
                a_arrival(s, b).wait_recv()

            for d in range(1, xs):
                x2_copy(s, d, b).start()

        near_field(s, 3)

        for j in range(2):

            @pl.loop(0, per_chunk)
            def _(i):
                b = j * per_chunk + i
                for d in range(1, xs):
                    x2_arrival(s, d, b).wait_recv()

            p2_copy(s, j, core).start()
        for j in range(2):
            inward(s, core * half + j * chunk, False)
        for j in range(2):
            p2_copy(s, j, 1 - core).wait_recv()
            inward(s, (1 - core) * half + j * chunk, j == 1)

        for i in range(reach):
            halo_copy(s, i, True).wait_send()
            halo_copy(s, i, False).wait_send()
        for j in range(2):
            pair_copy(s, j).wait_send()
            p2_copy(s, j, core).wait_send()
            for d in range(1, xs):
                x_copy(s, j, d).wait_send()

        @pl.loop(0, per_half)
        def _(b):
            for d in range(1, xs):
                x2_copy(s, d, b).wait_send()

            @pl.when(core * per_half + b != blk)
            def _():
                b_copy(s, b).wait_send()

        @pl.when(is_owner)
        def _():
            @pl.loop(1, blks)
            def _(o):
                a_copy(s, o).wait_send()

        @pl.when(s < ITERS - 1)
        def _():
            def solve_next(i, carry):
                p = solve_order(i)
                win[reach + p] = dot(src[p], t_ref[p], NT_DIMS).astype(BF16)
                return carry

            lax.fori_loop(0, reach, solve_next, 0)
            for batch in range(reach // 2):
                halo_send(s + 1, batch)
            lax.fori_loop(reach, count, solve_next, 0)

    def out_copy(p):
        return pltpu.make_async_copy(out_stage.at[p], out_hbm.at[p], out_sem.at[p])

    @pl.loop(0, count)
    def _(p):
        out_stage[p] = dot(src[p], t_ref[p], NT_DIMS).astype(BF16)
        out_copy(p).start()

    @pl.loop(0, count)
    def _(p):
        out_copy(p).wait()


def local(
    incident,
    t_matrices,
    translations,
    near_index,
    near_count,
    near_type,
    phases,
    wave_basis,
    grating_blocks,
):
    doms, blks = lax.axis_size("dom"), lax.axis_size("blk")
    xs = doms // 2
    count, width, rows_m = incident.shape
    turned = (count, rows_m, width)
    reach = count // 2
    kinds = translations.shape[0]
    most = near_index.shape[1]
    total = wave_basis.shape[0]
    half = total // 2
    order = grating_blocks.shape[1]
    part = rows_m // xs
    per_half = blks // 2
    hbm = pl.BlockSpec(memory_space=pl.ANY)
    smem = pl.BlockSpec(memory_space=pltpu.SMEM)
    sem = pltpu.SemaphoreType.DMA
    n = ITERS
    result = pl.pallas_call(
        functools.partial(kernel, xs),
        out_shape=jax.ShapeDtypeStruct(turned, BF16),
        in_specs=[smem] * 3 + [hbm] * 6,
        out_specs=hbm,
        scratch_shapes=[
            pltpu.SMEM((count, 2 * most + kinds), jnp.int32),
            pltpu.VMEM((count, total), BF16),
            pltpu.VMEM((count, 1, total), BF16),
            pltpu.VMEM((1, order, order), F32),
            pltpu.VMEM(turned, BF16),
            pltpu.VMEM(turned, BF16),
            pltpu.VMEM((count, width, width), BF16),
            pltpu.VMEM((kinds, width, width), BF16),
            pltpu.VMEM((total, width), BF16),
            pltpu.VMEM((count + 2 * reach, rows_m, width), BF16),
            pltpu.VMEM((n, 2 * reach, rows_m, width), BF16),
            pltpu.VMEM((count, rows_m, width), F32),
            pltpu.VMEM((count, rows_m, width), BF16),
            pltpu.VMEM((most + 1, rows_m, width), BF16),
            pltpu.VMEM((kinds, 2 * rows_m, width), BF16),
            pltpu.VMEM((n, rows_m, half), BF16),
            pltpu.VMEM((n, rows_m, half), BF16),
            pltpu.VMEM((n, rows_m, half), BF16),
            pltpu.VMEM((n, xs - 1, part, half), BF16),
            pltpu.VMEM((n, part, half), BF16),
            pltpu.VMEM((n, blks, part, order), BF16),
            pltpu.VMEM((n, rows_m, total), BF16),
            sem((count,)),
            sem((count,)),
            sem((4,)),
            sem((count,)),
            sem((n, 2)),
            sem((n, 2)),
            sem((n, 2, xs - 1)),
            sem((n, 2, xs - 1)),
            sem((n, per_half)),
            sem((n, blks)),
            sem((n, blks)),
            sem((n, per_half)),
            sem((n, xs - 1, per_half)),
            sem((n, xs - 1, per_half)),
            sem((n, 2)),
            sem((n, 2)),
            sem((n, 2 * reach)),
            sem((n, 2 * reach)),
        ],
        compiler_params=pltpu.CompilerParams(
            collective_id=0, has_side_effects=True, vmem_limit_bytes=60 * 2**20
        ),
    )(
        near_index,
        near_count,
        near_type,
        jnp.swapaxes(incident, 1, 2),
        t_matrices,
        translations,
        phases,
        wave_basis,
        grating_blocks,
    )
    return jnp.swapaxes(result, 1, 2)


def solution(mesh):
    placed = (
        P(("dom", "blk"), None, None),
        P(("dom", "blk"), None, None),
        P(),
        P(("dom", "blk"), None),
        P(("dom", "blk")),
        P(("dom", "blk"), None),
        P(("dom", "blk"), None),
        P(),
        P("blk", None, None),
    )
    return jax.shard_map(
        local, mesh=mesh, in_specs=placed, out_specs=P(("dom", "blk"), None, None), check_vma=False
    )
```

```python
import functools

import jax
import jax.numpy as jnp
from jax import lax
from jax.experimental import pallas as pl
from jax.experimental.pallas import tpu as pltpu
from jax.sharding import PartitionSpec as P

ITERS = 2
F32 = jnp.float32
BF16 = jnp.bfloat16
NT_DIMS = (((1,), (1,)), ((), ()))
NN_DIMS = (((1,), (0,)), ((), ()))


def dot(a, b, dims, precision=None):
    return lax.dot_general(a, b, dims, precision=precision, preferred_element_type=F32)


def kernel(
    xs,
    zs,
    index_ref,
    count_ref,
    type_ref,
    incident_hbm,
    t_hbm,
    moves_hbm,
    phases_hbm,
    basis_hbm,
    grating_hbm,
    out_hbm,
    table_ref,
    phases_flat,
    phases_ref,
    grating_ref,
    inc_ref,
    t_ref,
    moves_ref,
    basis_ref,
    win,
    halo,
    acc,
    src,
    steps,
    groups,
    pair_out,
    pair_in,
    x_out,
    x_in,
    b_out,
    b_in,
    refl,
    inc_sem,
    t_sem,
    load_sem,
    basis_sem,
    out_sem,
    pair_s,
    pair_r,
    x_s,
    x_r,
    b_s,
    b_r,
    a_s,
    a_r,
    x2_s,
    x2_r,
    p2_s,
    p2_r,
    halo_s,
    halo_r,
):
    count, rows_m, _ = inc_ref.shape
    reach = count // 2
    kinds = moves_ref.shape[0]
    most = index_ref.shape[1]
    width = basis_ref.shape[1]
    total = basis_ref.shape[0]
    half = total // 2
    chunk = half // 2
    order = grating_ref.shape[1]
    doms, blks = 2 * xs, total // order
    ys = blks // zs
    part = rows_m // xs

    dom = lax.axis_index("dom")
    blk = lax.axis_index("blk")
    x, core = dom // 2, lax.rem(dom, 2)
    z, y = blk // ys, lax.rem(blk, ys)
    partner = x * 2 + (1 - core)
    linear = dom * blks + blk
    after = lax.rem(linear + 1, doms * blks)
    before = lax.rem(linear + doms * blks - 1, doms * blks)
    after_id = (after // blks, lax.rem(after, blks))
    before_id = (before // blks, lax.rem(before, blks))

    is_owner = y // 2 == core

    def at_x(d):
        return lax.rem(x + d, xs)

    def at_z(d):
        return lax.rem(z + d, zs)

    def peer_x(d):
        return (at_x(d) * 2 + core, blk)

    def remote(source, target, send, recv, device):
        return pltpu.make_async_remote_copy(
            src_ref=source,
            dst_ref=target,
            send_sem=send,
            recv_sem=recv,
            device_id=device,
            device_id_type=pl.DeviceIdType.MESH,
        )

    def solve_order(i):
        return jnp.where(lax.rem(i, 2) == 0, count - 1 - i // 2, i // 2)

    def inc_load(p):
        return pltpu.make_async_copy(incident_hbm.at[p], inc_ref.at[p], inc_sem.at[p])

    def t_load(p):
        return pltpu.make_async_copy(t_hbm.at[p], t_ref.at[p], t_sem.at[p])

    @pl.loop(0, count)
    def _(i):
        p = solve_order(i)
        inc_load(p).start()
        t_load(p).start()

    def basis_load(q):
        b = lax.rem(q, zs) * ys + q // zs
        return pltpu.make_async_copy(
            basis_hbm.at[pl.ds(pl.multiple_of(b * order, order), order), :],
            basis_ref.at[pl.ds(pl.multiple_of(q * order, order), order), :],
            basis_sem.at[q],
        )

    moves_load = pltpu.make_async_copy(moves_hbm, moves_ref, load_sem.at[1])
    phases_load = pltpu.make_async_copy(phases_hbm, phases_flat, load_sem.at[2])
    grating_load = pltpu.make_async_copy(grating_hbm, grating_ref, load_sem.at[3])
    phases_load.start()
    grating_load.start()

    @pl.loop(0, blks)
    def _(q):
        basis_load(q).start()

    moves_load.start()

    barrier = pltpu.get_barrier_semaphore()

    def greet(device):
        pl.semaphore_signal(
            barrier, inc=1, device_id=device, device_id_type=pl.DeviceIdType.MESH
        )

    greet((partner, blk))

    for d in range(1, xs):
        greet(peer_x(d))

    @pl.loop(1, blks)
    def _(o):
        greet((dom, lax.rem(blk + o, blks)))

    greet(after_id)
    greet(before_id)

    steps[most] = jnp.zeros((rows_m, width), BF16)

    @pl.loop(0, count)
    def _(p):
        live = count_ref[p]
        slot = [
            jnp.clip(index_ref[p, k] - linear * count + reach, 0, count + 2 * reach - 1)
            for k in range(most)
        ]
        key = [jnp.where(k < live, type_ref[p, k], kinds) for k in range(most)]
        rank = [jnp.int32(0)] * most
        for k in range(most):
            for n in range(k + 1, most):
                later = (key[n] < key[k]).astype(jnp.int32)
                rank[k] = rank[k] + later
                rank[n] = rank[n] + (1 - later)
        sorted_slot, sorted_key = [], []
        for r in range(most):
            here, kind = slot[0], key[0]
            for k in range(1, most):
                hit = rank[k] == r
                here = jnp.where(hit, slot[k], here)
                kind = jnp.where(hit, key[k], kind)
            sorted_slot.append(here)
            sorted_key.append(kind)
        for r in range(most):
            table_ref[p, r] = sorted_slot[r]
            if r > 0:
                table_ref[p, most + r] = (sorted_key[r] == sorted_key[r - 1]).astype(jnp.int32)
        for t in range(kinds):
            last = jnp.int32(most)
            for r in range(most):
                last = jnp.where(sorted_key[r] == t, r, last)
            table_ref[p, 2 * most + t] = last

    def halo_copy(s, i, to_after):
        if to_after:
            return remote(
                win.at[2 * reach + i], halo.at[s, i], halo_s.at[s, i], halo_r.at[s, i], after_id
            )
        return remote(
            win.at[reach + i],
            halo.at[s, reach + i],
            halo_s.at[s, reach + i],
            halo_r.at[s, reach + i],
            before_id,
        )

    def halo_send(s, batch):
        halo_copy(s, reach - 1 - batch, True).start()
        halo_copy(s, batch, False).start()

    def solve_first(i, carry):
        p = solve_order(i)
        inc_load(p).wait()
        t_load(p).wait()
        win[reach + p] = dot(inc_ref[p], t_ref[p], NT_DIMS).astype(BF16)
        return carry

    lax.fori_loop(0, reach, solve_first, 0)
    pl.semaphore_wait(barrier, 1 + (blks - 1) + (xs - 1) + 2)
    halo_send(0, 0)
    lax.fori_loop(reach, count, solve_first, 0)
    phases_load.wait()
    for p in range(count):
        for q in range(blks):
            b = (q % zs) * ys + q // zs
            phases_ref[p, :, q * order : (q + 1) * order] = phases_flat[
                p : p + 1, b * order : (b + 1) * order
            ]

    @pl.loop(0, blks)
    def _(q):
        basis_load(q).wait()

    def near_field(s, batch):
        lo, hi = reach - 1 - batch, reach + batch
        halo_copy(s, reach - 1 - batch, True).wait_recv()
        halo_copy(s, batch, False).wait_recv()
        win[lo] = halo[s, lo]
        win[3 * reach + batch] = halo[s, reach + batch]
        piece = 32 if rows_m % 32 == 0 else rows_m
        for place, p in enumerate((lo, hi)):
            index = [table_ref[p, k] for k in range(most)]
            same = [table_ref[p, most + k].astype(F32) if k else None for k in range(most)]
            ends = [table_ref[p, 2 * most + t] for t in range(kinds)]

            @pl.loop(0, rows_m // piece)
            def _(r):
                rows = pl.ds(pl.multiple_of(r * piece, piece), piece)
                run = win[index[0], rows, :].astype(F32)
                steps[0, rows, :] = run.astype(BF16)
                for k in range(1, most):
                    run = run * same[k] + win[index[k], rows, :].astype(F32)
                    steps[k, rows, :] = run.astype(BF16)

            for t in range(kinds):
                groups[t, place * rows_m : (place + 1) * rows_m, :] = steps[ends[t]]
        field = dot(groups[0], moves_ref[0], NT_DIMS)
        for t in range(1, kinds):
            field = field + dot(groups[t], moves_ref[t], NT_DIMS)
        for place, p in enumerate((lo, hi)):
            acc[p] = inc_ref[p].astype(F32) + field[place * rows_m : (place + 1) * rows_m]

    my_rows = pl.ds(pl.multiple_of(x * part, part), part)

    def outward(start):
        cols = pl.ds(pl.multiple_of(start, chunk), chunk)
        spread = dot(
            win[reach : reach + count].reshape(count * rows_m, width), basis_ref[cols, :], NT_DIMS
        ).reshape(count, rows_m, chunk)
        return jnp.sum(spread * phases_ref[:, :, cols].astype(F32), axis=0)

    def inward(s, rows, start, last):
        cols = pl.ds(pl.multiple_of(start, half), half)
        weighted = (refl[s, rows, cols][None] * phases_ref[:, :, cols]).reshape(count * part, half)
        back = dot(weighted, basis_ref[cols, :], NN_DIMS).reshape(count, part, width)
        if last:
            src[:, rows, :] = (acc[:, rows, :] + back).astype(BF16)
        else:
            acc[:, rows, :] += back

    def columns(start, size):
        return pl.ds(pl.multiple_of(start, order), size)

    def x_rows(i):
        return pl.ds(pl.multiple_of(i * part, part), part)

    def chunk_cols(j):
        return columns(j * chunk, chunk)

    def pair_copy(s, j):
        return remote(
            pair_out.at[s, :, chunk_cols(j)],
            pair_in.at[s, :, chunk_cols(j)],
            pair_s.at[s, j],
            pair_r.at[s, j],
            (partner, blk),
        )

    def x_copy(s, j, d):
        return remote(
            x_out.at[s, x_rows(at_x(d)), chunk_cols(j)],
            x_in.at[s, d - 1, :, chunk_cols(j)],
            x_s.at[s, j, d - 1],
            x_r.at[s, j, d - 1],
            peer_x(d),
        )

    def owner(j, d):
        return at_z(d) * ys + 2 * core + j

    def b_copy(s, j, d):
        return remote(
            b_out.at[s, :, columns(j * chunk + at_z(d) * order, order)],
            b_in.at[s, blk],
            b_s.at[s, j, d],
            b_r.at[s, blk],
            (dom, owner(j, d)),
        )

    def b_arrival(s, i):
        return remote(b_in.at[s, i], b_in.at[s, i], b_s.at[s, 0, 0], b_r.at[s, i], (dom, i))

    def block(s, rows, at_y, z_of):
        return refl.at[s, rows, columns((at_y * zs + z_of) * order, order)]

    def a_copy(s, o):
        here = block(s, x_rows(x), y, z)
        sem = a_r.at[s, lax.rem(y, 2), z]
        return remote(here, here, a_s.at[s, o], sem, (dom, lax.rem(blk + o, blks)))

    def a_arrival(s, j, d):
        here = block(s, x_rows(x), 2 * core + j, at_z(d))
        return remote(here, here, a_s.at[s, 0], a_r.at[s, j, at_z(d)], (dom, owner(j, d)))

    def x2_copy(s, j, d, e):
        here = block(s, x_rows(x), 2 * core + j, at_z(e))
        sem = (s, d - 1, j, at_z(e))
        return remote(here, here, x2_s.at[sem], x2_r.at[sem], peer_x(d))

    def x2_arrival(s, j, d, i):
        here = block(s, x_rows(at_x(xs - d)), 2 * core + j, i)
        sem = (s, d - 1, j, i)
        return remote(here, here, x2_s.at[sem], x2_r.at[sem], peer_x(xs - d))

    def p2_copy(s, d, sender):
        here = refl.at[s, x_rows(at_x(xs - d)), pl.ds(pl.multiple_of(sender * half, half), half)]
        return remote(here, here, p2_s.at[s, d], p2_r.at[s, d], (partner, blk))

    def near_first(n):
        return sorted(range(n), key=lambda d: (min(d, n - d), d))

    def launch(s):
        @pl.loop(0, 2)
        def _(j):
            pair_out[s, :, chunk_cols(j)] = outward((1 - core) * half + j * chunk).astype(BF16)
            pair_copy(s, j).start()

        @pl.loop(0, 2)
        def _(j):
            cols = chunk_cols(j)
            own = outward(core * half + j * chunk)
            pair_copy(s, j).wait_recv()
            x_out[s, :, cols] = (own + pair_in[s, :, cols].astype(F32)).astype(BF16)
            for d in near_first(xs)[:0:-1]:
                x_copy(s, j, d).start()

    launch(0)
    halo_send(0, 1)
    moves_load.wait()
    grating_load.wait()

    @pl.loop(0, ITERS)
    def _(s):
        near_field(s, 0)

        for j in range(2):
            both = x_out[s, x_rows(x), chunk_cols(j)].astype(F32)
            for d in range(1, xs):
                x_copy(s, j, d).wait_recv()
                both = both + x_in[s, d - 1, :, chunk_cols(j)].astype(F32)
            b_out[s, :, chunk_cols(j)] = both.astype(BF16)
            for d in near_first(zs)[::-1]:

                @pl.when(owner(j, d) != blk)
                def _():
                    b_copy(s, j, d).start()

        halo_send(s, 2)
        near_field(s, 1)

        @pl.when(is_owner)
        def _():
            def gather(o, so_far):
                i = lax.rem(blk + o, blks)
                b_arrival(s, i).wait_recv()
                return so_far + b_in[s, i].astype(F32)

            own = b_out[s, :, columns(lax.rem(y, 2) * chunk + z * order, order)].astype(F32)
            sums = lax.fori_loop(1, blks, gather, own)
            result = dot(sums, grating_ref[0], NT_DIMS, lax.Precision.HIGHEST)
            refl[s, x_rows(x), columns((y * zs + z) * order, order)] = result.astype(BF16)

            @pl.loop(1, blks)
            def _(o):
                a_copy(s, o).start()

        halo_send(s, 3)
        near_field(s, 2)

        for e in near_first(zs):
            for j in range(2):

                @pl.when(owner(j, e) != blk)
                def _():
                    a_arrival(s, j, e).wait_recv()

                for d in near_first(xs)[:0:-1]:
                    x2_copy(s, j, d, e).start()
        p2_copy(s, 0, core).start()

        near_field(s, 3)

        def inward_own(d):
            inward(s, x_rows(at_x(xs - d)), core * half, False)

        def inward_other(d):
            p2_copy(s, d, 1 - core).wait_recv()
            inward(s, x_rows(at_x(xs - d)), (1 - core) * half, True)

        turn = near_first(xs)
        inward_own(turn[0])
        for n, d in enumerate(turn[1:]):
            for j in range(2):
                for i in range(zs):
                    x2_arrival(s, j, d, i).wait_recv()
            p2_copy(s, d, core).start()
            inward_own(d)
            inward_other(turn[n])
        inward_other(turn[-1])

        for i in range(reach):
            halo_copy(s, i, True).wait_send()
            halo_copy(s, i, False).wait_send()
        for j in range(2):
            pair_copy(s, j).wait_send()
            for d in range(zs):

                @pl.when(owner(j, d) != blk)
                def _():
                    b_copy(s, j, d).wait_send()

            for d in range(1, xs):
                x_copy(s, j, d).wait_send()
                for e in range(zs):
                    x2_copy(s, j, d, e).wait_send()
        for d in range(xs):
            p2_copy(s, d, core).wait_send()

        @pl.when(is_owner)
        def _():
            @pl.loop(1, blks)
            def _(o):
                a_copy(s, o).wait_send()

        @pl.when(s < ITERS - 1)
        def _():
            def solve_next(i, carry):
                p = solve_order(i)
                win[reach + p] = dot(src[p], t_ref[p], NT_DIMS).astype(BF16)
                return carry

            lax.fori_loop(0, count - 2, solve_next, 0)
            halo_send(s + 1, 0)
            lax.fori_loop(count - 2, count, solve_next, 0)
            launch(s + 1)
            halo_send(s + 1, 1)

    out = pltpu.make_async_copy(src, out_hbm, out_sem.at[0])
    out.start()
    out.wait()


def last_solve(src_hbm, t_hbm, out_hbm, src, t_ref, out, src_sem, t_sem, out_sem):
    count = src.shape[0]

    def load(p):
        return (
            pltpu.make_async_copy(src_hbm.at[p], src.at[p], src_sem.at[p]),
            pltpu.make_async_copy(t_hbm.at[p], t_ref.at[p], t_sem.at[p]),
        )

    def store(p):
        return pltpu.make_async_copy(out.at[p], out_hbm.at[p], out_sem.at[p])

    @pl.loop(0, count)
    def _(p):
        for copy in load(p):
            copy.start()

    @pl.loop(0, count)
    def _(p):
        for copy in load(p):
            copy.wait()
        out[p] = dot(src[p], t_ref[p], NT_DIMS).astype(BF16)
        store(p).start()

    @pl.loop(0, count)
    def _(p):
        store(p).wait()


def local(
    incident,
    t_matrices,
    translations,
    near_index,
    near_count,
    near_type,
    phases,
    wave_basis,
    grating_blocks,
):
    doms, blks = lax.axis_size("dom"), lax.axis_size("blk")
    xs = doms // 2
    zs = xs
    ys = blks // zs
    count, width, rows_m = incident.shape
    turned = (count, rows_m, width)
    reach = count // 2
    kinds = translations.shape[0]
    most = near_index.shape[1]
    total = wave_basis.shape[0]
    half = total // 2
    chunk = half // 2
    order = grating_blocks.shape[1]
    part = rows_m // xs
    hbm = pl.BlockSpec(memory_space=pl.ANY)
    smem = pl.BlockSpec(memory_space=pltpu.SMEM)
    sem = pltpu.SemaphoreType.DMA
    n = ITERS
    source = pl.pallas_call(
        functools.partial(kernel, xs, zs),
        out_shape=jax.ShapeDtypeStruct(turned, BF16),
        in_specs=[smem] * 3 + [hbm] * 6,
        out_specs=hbm,
        scratch_shapes=[
            pltpu.SMEM((count, 2 * most + kinds), jnp.int32),
            pltpu.VMEM((count, total), BF16),
            pltpu.VMEM((count, 1, total), BF16),
            pltpu.VMEM((1, order, order), F32),
            pltpu.VMEM(turned, BF16),
            pltpu.VMEM((count, width, width), BF16),
            pltpu.VMEM((kinds, width, width), BF16),
            pltpu.VMEM((total, width), BF16),
            pltpu.VMEM((count + 2 * reach, rows_m, width), BF16),
            pltpu.VMEM((n, 2 * reach, rows_m, width), BF16),
            pltpu.VMEM((count, rows_m, width), F32),
            pltpu.VMEM((count, rows_m, width), BF16),
            pltpu.VMEM((most + 1, rows_m, width), BF16),
            pltpu.VMEM((kinds, 2 * rows_m, width), BF16),
            pltpu.VMEM((n, rows_m, half), BF16),
            pltpu.VMEM((n, rows_m, half), BF16),
            pltpu.VMEM((n, rows_m, half), BF16),
            pltpu.VMEM((n, xs - 1, part, half), BF16),
            pltpu.VMEM((n, part, half), BF16),
            pltpu.VMEM((n, blks, part, order), BF16),
            pltpu.VMEM((n, rows_m, total), BF16),
            sem((count,)),
            sem((count,)),
            sem((4,)),
            sem((blks,)),
            sem((1,)),
            sem((n, 2)),
            sem((n, 2)),
            sem((n, 2, xs - 1)),
            sem((n, 2, xs - 1)),
            sem((n, 2, zs)),
            sem((n, blks)),
            sem((n, blks)),
            sem((n, 2, zs)),
            sem((n, xs - 1, 2, zs)),
            sem((n, xs - 1, 2, zs)),
            sem((n, xs)),
            sem((n, xs)),
            sem((n, 2 * reach)),
            sem((n, 2 * reach)),
        ],
        compiler_params=pltpu.CompilerParams(
            collective_id=0, has_side_effects=True, vmem_limit_bytes=60 * 2**20
        ),
    )(
        near_index,
        near_count,
        near_type,
        jnp.swapaxes(incident, 1, 2),
        t_matrices,
        translations,
        phases,
        wave_basis,
        grating_blocks,
    )
    result = pl.pallas_call(
        last_solve,
        out_shape=jax.ShapeDtypeStruct(turned, BF16),
        in_specs=[hbm] * 2,
        out_specs=hbm,
        scratch_shapes=[
            pltpu.VMEM(turned, BF16),
            pltpu.VMEM((count, width, width), BF16),
            pltpu.VMEM(turned, BF16),
            sem((count,)),
            sem((count,)),
            sem((count,)),
        ],
        compiler_params=pltpu.CompilerParams(vmem_limit_bytes=60 * 2**20),
    )(source, t_matrices)
    return jnp.swapaxes(result, 1, 2)


def solution(mesh):
    placed = (
        P(("dom", "blk"), None, None),
        P(("dom", "blk"), None, None),
        P(),
        P(("dom", "blk"), None),
        P(("dom", "blk")),
        P(("dom", "blk"), None),
        P(("dom", "blk"), None),
        P(),
        P("blk", None, None),
    )
    return jax.shard_map(
        local, mesh=mesh, in_specs=placed, out_specs=P(("dom", "blk"), None, None), check_vma=False
    )
```

```python
import functools

import jax
import jax.numpy as jnp
from jax import lax
from jax.experimental import pallas as pl
from jax.experimental.pallas import tpu as pltpu
from jax.sharding import PartitionSpec as P

ITERS = 2
F32 = jnp.float32
BF16 = jnp.bfloat16
NT_DIMS = (((1,), (1,)), ((), ()))
NN_DIMS = (((1,), (0,)), ((), ()))


def dot(a, b, dims, precision=None):
    return lax.dot_general(a, b, dims, precision=precision, preferred_element_type=F32)


def kernel(
    xs,
    zs,
    index_ref,
    count_ref,
    type_ref,
    incident_hbm,
    t_hbm,
    moves_hbm,
    phases_hbm,
    basis_hbm,
    grating_hbm,
    out_hbm,
    table_ref,
    phases_flat,
    phases_ref,
    grating_ref,
    inc_ref,
    t_ref,
    moves_ref,
    basis_ref,
    win,
    halo,
    acc,
    src,
    steps,
    groups,
    pair_out,
    pair_in,
    x_out,
    x_in,
    b_out,
    b_in,
    refl,
    inc_sem,
    t_sem,
    load_sem,
    basis_sem,
    out_sem,
    pair_s,
    pair_r,
    x_s,
    x_r,
    b_s,
    b_r,
    a_s,
    a_r,
    x2_s,
    x2_r,
    p2_s,
    p2_r,
    halo_s,
    halo_r,
):
    count, rows_m, _ = inc_ref.shape
    reach = count // 2
    kinds = moves_ref.shape[0]
    most = index_ref.shape[1]
    width = basis_ref.shape[1]
    total = basis_ref.shape[0]
    half = total // 2
    chunk = half // 2
    order = grating_ref.shape[1]
    doms, blks = 2 * xs, total // order
    ys = blks // zs
    part = rows_m // xs

    dom = lax.axis_index("dom")
    blk = lax.axis_index("blk")
    x, core = dom // 2, lax.rem(dom, 2)
    z, y = blk // ys, lax.rem(blk, ys)
    partner = x * 2 + (1 - core)
    linear = dom * blks + blk
    after = lax.rem(linear + 1, doms * blks)
    before = lax.rem(linear + doms * blks - 1, doms * blks)
    after_id = (after // blks, lax.rem(after, blks))
    before_id = (before // blks, lax.rem(before, blks))

    is_owner = y // 2 == core

    def at_x(d):
        return lax.rem(x + d, xs)

    def at_z(d):
        return lax.rem(z + d, zs)

    def peer_x(d):
        return (at_x(d) * 2 + core, blk)

    def remote(source, target, send, recv, device):
        return pltpu.make_async_remote_copy(
            src_ref=source,
            dst_ref=target,
            send_sem=send,
            recv_sem=recv,
            device_id=device,
            device_id_type=pl.DeviceIdType.MESH,
        )

    def solve_order(i):
        return jnp.where(lax.rem(i, 2) == 0, count - 1 - i // 2, i // 2)

    def inc_load(p):
        return pltpu.make_async_copy(incident_hbm.at[p], inc_ref.at[p], inc_sem.at[p])

    def t_load(p):
        return pltpu.make_async_copy(t_hbm.at[p], t_ref.at[p], t_sem.at[p])

    @pl.loop(0, count)
    def _(i):
        p = solve_order(i)
        inc_load(p).start()
        t_load(p).start()

    def basis_load(q):
        b = lax.rem(q, zs) * ys + q // zs
        return pltpu.make_async_copy(
            basis_hbm.at[pl.ds(pl.multiple_of(b * order, order), order), :],
            basis_ref.at[pl.ds(pl.multiple_of(q * order, order), order), :],
            basis_sem.at[q],
        )

    moves_load = pltpu.make_async_copy(moves_hbm, moves_ref, load_sem.at[1])
    phases_load = pltpu.make_async_copy(phases_hbm, phases_flat, load_sem.at[2])
    grating_load = pltpu.make_async_copy(grating_hbm, grating_ref, load_sem.at[3])
    phases_load.start()
    grating_load.start()

    @pl.loop(0, blks)
    def _(q):
        basis_load(q).start()

    moves_load.start()

    barrier = pltpu.get_barrier_semaphore()

    def greet(device):
        pl.semaphore_signal(
            barrier, inc=1, device_id=device, device_id_type=pl.DeviceIdType.MESH
        )

    greet((partner, blk))

    for d in range(1, xs):
        greet(peer_x(d))

    @pl.loop(1, blks)
    def _(o):
        greet((dom, lax.rem(blk + o, blks)))

    greet(after_id)
    greet(before_id)

    steps[most] = jnp.zeros((rows_m, width), BF16)

    @pl.loop(0, count)
    def _(p):
        live = count_ref[p]
        slot = [
            jnp.clip(index_ref[p, k] - linear * count + reach, 0, count + 2 * reach - 1)
            for k in range(most)
        ]
        key = [jnp.where(k < live, type_ref[p, k], kinds) for k in range(most)]
        rank = [jnp.int32(0)] * most
        for k in range(most):
            for n in range(k + 1, most):
                later = (key[n] < key[k]).astype(jnp.int32)
                rank[k] = rank[k] + later
                rank[n] = rank[n] + (1 - later)
        sorted_slot, sorted_key = [], []
        for r in range(most):
            here, kind = slot[0], key[0]
            for k in range(1, most):
                hit = rank[k] == r
                here = jnp.where(hit, slot[k], here)
                kind = jnp.where(hit, key[k], kind)
            sorted_slot.append(here)
            sorted_key.append(kind)
        for r in range(most):
            table_ref[p, r] = sorted_slot[r]
            if r > 0:
                table_ref[p, most + r] = (sorted_key[r] == sorted_key[r - 1]).astype(jnp.int32)
        for t in range(kinds):
            last = jnp.int32(most)
            for r in range(most):
                last = jnp.where(sorted_key[r] == t, r, last)
            table_ref[p, 2 * most + t] = last

    def halo_copy(s, i, to_after):
        if to_after:
            return remote(
                win.at[2 * reach + i], halo.at[s, i], halo_s.at[s, i], halo_r.at[s, i], after_id
            )
        return remote(
            win.at[reach + i],
            halo.at[s, reach + i],
            halo_s.at[s, reach + i],
            halo_r.at[s, reach + i],
            before_id,
        )

    def halo_send(s, batch):
        halo_copy(s, reach - 1 - batch, True).start()
        halo_copy(s, batch, False).start()

    def solve_first(i, carry):
        p = solve_order(i)
        inc_load(p).wait()
        t_load(p).wait()
        win[reach + p] = dot(inc_ref[p], t_ref[p], NT_DIMS).astype(BF16)
        return carry

    lax.fori_loop(0, reach, solve_first, 0)
    pl.semaphore_wait(barrier, 1 + (blks - 1) + (xs - 1) + 2)
    halo_send(0, 0)
    lax.fori_loop(reach, count, solve_first, 0)
    phases_load.wait()
    for p in range(count):
        for q in range(blks):
            b = (q % zs) * ys + q // zs
            phases_ref[p, :, q * order : (q + 1) * order] = phases_flat[
                p : p + 1, b * order : (b + 1) * order
            ]

    @pl.loop(0, blks)
    def _(q):
        basis_load(q).wait()

    def near_field(s, batch):
        lo, hi = reach - 1 - batch, reach + batch
        halo_copy(s, reach - 1 - batch, True).wait_recv()
        halo_copy(s, batch, False).wait_recv()
        win[lo] = halo[s, lo]
        win[3 * reach + batch] = halo[s, reach + batch]
        piece = 32 if rows_m % 32 == 0 else rows_m
        for place, p in enumerate((lo, hi)):
            index = [table_ref[p, k] for k in range(most)]
            same = [table_ref[p, most + k].astype(F32) if k else None for k in range(most)]
            ends = [table_ref[p, 2 * most + t] for t in range(kinds)]

            @pl.loop(0, rows_m // piece)
            def _(r):
                rows = pl.ds(pl.multiple_of(r * piece, piece), piece)
                run = win[index[0], rows, :].astype(F32)
                steps[0, rows, :] = run.astype(BF16)
                for k in range(1, most):
                    run = run * same[k] + win[index[k], rows, :].astype(F32)
                    steps[k, rows, :] = run.astype(BF16)

            for t in range(kinds):
                groups[t, place * rows_m : (place + 1) * rows_m, :] = steps[ends[t]]
        field = dot(groups[0], moves_ref[0], NT_DIMS)
        for t in range(1, kinds):
            field = field + dot(groups[t], moves_ref[t], NT_DIMS)
        for place, p in enumerate((lo, hi)):
            acc[p] = inc_ref[p].astype(F32) + field[place * rows_m : (place + 1) * rows_m]

    my_rows = pl.ds(pl.multiple_of(x * part, part), part)

    def outward(start):
        cols = pl.ds(pl.multiple_of(start, chunk), chunk)
        spread = dot(
            win[reach : reach + count].reshape(count * rows_m, width), basis_ref[cols, :], NT_DIMS
        ).reshape(count, rows_m, chunk)
        return jnp.sum(spread * phases_ref[:, :, cols].astype(F32), axis=0)

    def inward(s, rows, start, last):
        cols = pl.ds(pl.multiple_of(start, half), half)
        weighted = (refl[s, rows, cols][None] * phases_ref[:, :, cols]).reshape(count * part, half)
        back = dot(weighted, basis_ref[cols, :], NN_DIMS).reshape(count, part, width)
        if last:
            src[:, rows, :] = (acc[:, rows, :] + back).astype(BF16)
        else:
            acc[:, rows, :] += back

    def columns(start, size):
        return pl.ds(pl.multiple_of(start, order), size)

    def x_rows(i):
        return pl.ds(pl.multiple_of(i * part, part), part)

    def chunk_cols(j):
        return columns(j * chunk, chunk)

    def pair_copy(s, j):
        return remote(
            pair_out.at[s, :, chunk_cols(j)],
            pair_in.at[s, :, chunk_cols(j)],
            pair_s.at[s, j],
            pair_r.at[s, j],
            (partner, blk),
        )

    def x_copy(s, j, d):
        return remote(
            x_out.at[s, x_rows(at_x(d)), chunk_cols(j)],
            x_in.at[s, d - 1, :, chunk_cols(j)],
            x_s.at[s, j, d - 1],
            x_r.at[s, j, d - 1],
            peer_x(d),
        )

    def owner(j, d):
        return at_z(d) * ys + 2 * core + j

    def b_copy(s, j, d):
        return remote(
            b_out.at[s, :, columns(j * chunk + at_z(d) * order, order)],
            b_in.at[s, blk],
            b_s.at[s, j, d],
            b_r.at[s, blk],
            (dom, owner(j, d)),
        )

    def b_arrival(s, i):
        return remote(b_in.at[s, i], b_in.at[s, i], b_s.at[s, 0, 0], b_r.at[s, i], (dom, i))

    def block(s, rows, at_y, z_of):
        return refl.at[s, rows, columns((at_y * zs + z_of) * order, order)]

    def a_copy(s, o):
        here = block(s, x_rows(x), y, z)
        sem = a_r.at[s, lax.rem(y, 2), z]
        return remote(here, here, a_s.at[s, o], sem, (dom, lax.rem(blk + o, blks)))

    def a_arrival(s, j, d):
        here = block(s, x_rows(x), 2 * core + j, at_z(d))
        return remote(here, here, a_s.at[s, 0], a_r.at[s, j, at_z(d)], (dom, owner(j, d)))

    def x2_copy(s, j, d, e):
        here = block(s, x_rows(x), 2 * core + j, at_z(e))
        sem = (s, d - 1, j, at_z(e))
        return remote(here, here, x2_s.at[sem], x2_r.at[sem], peer_x(d))

    def x2_arrival(s, j, d, i):
        here = block(s, x_rows(at_x(xs - d)), 2 * core + j, i)
        sem = (s, d - 1, j, i)
        return remote(here, here, x2_s.at[sem], x2_r.at[sem], peer_x(xs - d))

    def p2_copy(s, d, sender):
        here = refl.at[s, x_rows(at_x(xs - d)), pl.ds(pl.multiple_of(sender * half, half), half)]
        return remote(here, here, p2_s.at[s, d], p2_r.at[s, d], (partner, blk))

    def near_first(n):
        return sorted(range(n), key=lambda d: (min(d, n - d), d))

    def launch(s):
        @pl.loop(0, 2)
        def _(j):
            pair_out[s, :, chunk_cols(j)] = outward((1 - core) * half + j * chunk).astype(BF16)
            pair_copy(s, j).start()

        @pl.loop(0, 2)
        def _(j):
            cols = chunk_cols(j)
            own = outward(core * half + j * chunk)
            pair_copy(s, j).wait_recv()
            x_out[s, :, cols] = (own + pair_in[s, :, cols].astype(F32)).astype(BF16)
            for d in near_first(xs)[:0:-1]:
                x_copy(s, j, d).start()

    launch(0)
    halo_send(0, 1)
    moves_load.wait()
    grating_load.wait()

    @pl.loop(0, ITERS)
    def _(s):
        near_field(s, 0)

        for j in range(2):
            both = x_out[s, x_rows(x), chunk_cols(j)].astype(F32)
            for d in range(1, xs):
                x_copy(s, j, d).wait_recv()
                both = both + x_in[s, d - 1, :, chunk_cols(j)].astype(F32)
            b_out[s, :, chunk_cols(j)] = both.astype(BF16)
            for d in near_first(zs)[::-1]:

                @pl.when(owner(j, d) != blk)
                def _():
                    b_copy(s, j, d).start()

        halo_send(s, 2)
        near_field(s, 1)

        @pl.when(is_owner)
        def _():
            def gather(o, so_far):
                i = lax.rem(blk + o, blks)
                b_arrival(s, i).wait_recv()
                return so_far + b_in[s, i].astype(F32)

            own = b_out[s, :, columns(lax.rem(y, 2) * chunk + z * order, order)].astype(F32)
            sums = lax.fori_loop(1, blks, gather, own)
            result = dot(sums, grating_ref[0], NT_DIMS, lax.Precision.HIGHEST)
            refl[s, x_rows(x), columns((y * zs + z) * order, order)] = result.astype(BF16)

            @pl.loop(1, blks)
            def _(o):
                a_copy(s, o).start()

        halo_send(s, 3)
        near_field(s, 2)

        for e in near_first(zs):
            for j in range(2):

                @pl.when(owner(j, e) != blk)
                def _():
                    a_arrival(s, j, e).wait_recv()

                for d in near_first(xs)[:0:-1]:
                    x2_copy(s, j, d, e).start()
        p2_copy(s, 0, core).start()

        near_field(s, 3)

        def inward_own(d):
            inward(s, x_rows(at_x(xs - d)), core * half, False)

        def inward_other(d):
            p2_copy(s, d, 1 - core).wait_recv()
            inward(s, x_rows(at_x(xs - d)), (1 - core) * half, True)

        turn = near_first(xs)
        inward_own(turn[0])
        for n, d in enumerate(turn[1:]):
            for j in range(2):
                for i in range(zs):
                    x2_arrival(s, j, d, i).wait_recv()
            p2_copy(s, d, core).start()
            inward_own(d)
            inward_other(turn[n])
        inward_other(turn[-1])

        for i in range(reach):
            halo_copy(s, i, True).wait_send()
            halo_copy(s, i, False).wait_send()
        @pl.when(s < ITERS - 1)
        def _():
            def solve_next(i, carry):
                p = solve_order(i)
                win[reach + p] = dot(src[p], t_ref[p], NT_DIMS).astype(BF16)
                return carry

            lax.fori_loop(0, count - 2, solve_next, 0)
            halo_send(s + 1, 0)
            lax.fori_loop(count - 2, count, solve_next, 0)
            launch(s + 1)
            halo_send(s + 1, 1)

        for j in range(2):
            pair_copy(s, j).wait_send()
            for d in range(zs):

                @pl.when(owner(j, d) != blk)
                def _():
                    b_copy(s, j, d).wait_send()

            for d in range(1, xs):
                x_copy(s, j, d).wait_send()
                for e in range(zs):
                    x2_copy(s, j, d, e).wait_send()
        for d in range(xs):
            p2_copy(s, d, core).wait_send()

        @pl.when(is_owner)
        def _():
            @pl.loop(1, blks)
            def _(o):
                a_copy(s, o).wait_send()

    out = pltpu.make_async_copy(src, out_hbm, out_sem.at[0])
    out.start()
    out.wait()


def last_solve(src_hbm, t_hbm, out_hbm, src, t_ref, out, src_sem, t_sem, out_sem):
    count = src.shape[0]

    def load(p):
        return (
            pltpu.make_async_copy(src_hbm.at[p], src.at[p], src_sem.at[p]),
            pltpu.make_async_copy(t_hbm.at[p], t_ref.at[p], t_sem.at[p]),
        )

    def store(p):
        return pltpu.make_async_copy(out.at[p], out_hbm.at[p], out_sem.at[p])

    @pl.loop(0, count)
    def _(p):
        for copy in load(p):
            copy.start()

    @pl.loop(0, count)
    def _(p):
        for copy in load(p):
            copy.wait()
        out[p] = dot(src[p], t_ref[p], NT_DIMS).astype(BF16)
        store(p).start()

    @pl.loop(0, count)
    def _(p):
        store(p).wait()


def local(
    incident,
    t_matrices,
    translations,
    near_index,
    near_count,
    near_type,
    phases,
    wave_basis,
    grating_blocks,
):
    doms, blks = lax.axis_size("dom"), lax.axis_size("blk")
    xs = doms // 2
    zs = xs
    ys = blks // zs
    count, width, rows_m = incident.shape
    turned = (count, rows_m, width)
    reach = count // 2
    kinds = translations.shape[0]
    most = near_index.shape[1]
    total = wave_basis.shape[0]
    half = total // 2
    chunk = half // 2
    order = grating_blocks.shape[1]
    part = rows_m // xs
    hbm = pl.BlockSpec(memory_space=pl.ANY)
    smem = pl.BlockSpec(memory_space=pltpu.SMEM)
    sem = pltpu.SemaphoreType.DMA
    n = ITERS
    source = pl.pallas_call(
        functools.partial(kernel, xs, zs),
        out_shape=jax.ShapeDtypeStruct(turned, BF16),
        in_specs=[smem] * 3 + [hbm] * 6,
        out_specs=hbm,
        scratch_shapes=[
            pltpu.SMEM((count, 2 * most + kinds), jnp.int32),
            pltpu.VMEM((count, total), BF16),
            pltpu.VMEM((count, 1, total), BF16),
            pltpu.VMEM((1, order, order), F32),
            pltpu.VMEM(turned, BF16),
            pltpu.VMEM((count, width, width), BF16),
            pltpu.VMEM((kinds, width, width), BF16),
            pltpu.VMEM((total, width), BF16),
            pltpu.VMEM((count + 2 * reach, rows_m, width), BF16),
            pltpu.VMEM((n, 2 * reach, rows_m, width), BF16),
            pltpu.VMEM((count, rows_m, width), F32),
            pltpu.VMEM((count, rows_m, width), BF16),
            pltpu.VMEM((most + 1, rows_m, width), BF16),
            pltpu.VMEM((kinds, 2 * rows_m, width), BF16),
            pltpu.VMEM((n, rows_m, half), BF16),
            pltpu.VMEM((n, rows_m, half), BF16),
            pltpu.VMEM((n, rows_m, half), BF16),
            pltpu.VMEM((n, xs - 1, part, half), BF16),
            pltpu.VMEM((n, part, half), BF16),
            pltpu.VMEM((n, blks, part, order), BF16),
            pltpu.VMEM((n, rows_m, total), BF16),
            sem((count,)),
            sem((count,)),
            sem((4,)),
            sem((blks,)),
            sem((1,)),
            sem((n, 2)),
            sem((n, 2)),
            sem((n, 2, xs - 1)),
            sem((n, 2, xs - 1)),
            sem((n, 2, zs)),
            sem((n, blks)),
            sem((n, blks)),
            sem((n, 2, zs)),
            sem((n, xs - 1, 2, zs)),
            sem((n, xs - 1, 2, zs)),
            sem((n, xs)),
            sem((n, xs)),
            sem((n, 2 * reach)),
            sem((n, 2 * reach)),
        ],
        compiler_params=pltpu.CompilerParams(
            collective_id=0, has_side_effects=True, vmem_limit_bytes=60 * 2**20
        ),
    )(
        near_index,
        near_count,
        near_type,
        jnp.swapaxes(incident, 1, 2),
        t_matrices,
        translations,
        phases,
        wave_basis,
        grating_blocks,
    )
    result = pl.pallas_call(
        last_solve,
        out_shape=jax.ShapeDtypeStruct(turned, BF16),
        in_specs=[hbm] * 2,
        out_specs=hbm,
        scratch_shapes=[
            pltpu.VMEM(turned, BF16),
            pltpu.VMEM((count, width, width), BF16),
            pltpu.VMEM(turned, BF16),
            sem((count,)),
            sem((count,)),
            sem((count,)),
        ],
        compiler_params=pltpu.CompilerParams(vmem_limit_bytes=60 * 2**20),
    )(source, t_matrices)
    return jnp.swapaxes(result, 1, 2)


def solution(mesh):
    placed = (
        P(("dom", "blk"), None, None),
        P(("dom", "blk"), None, None),
        P(),
        P(("dom", "blk"), None),
        P(("dom", "blk")),
        P(("dom", "blk"), None),
        P(("dom", "blk"), None),
        P(),
        P("blk", None, None),
    )
    return jax.shard_map(
        local, mesh=mesh, in_specs=placed, out_specs=P(("dom", "blk"), None, None), check_vma=False
    )
```
